32 devices in a mesh: groups: 2 (over y), seq: 4 (over z), head: 4 (over x, core).
Axes of the slice: x: 2, y: 2, z: 4, core: 2. Of those that a mesh axis runs over, the one named last changes fastest.
Arguments:
- tokens: bfloat16 [4096, 4096], P(('groups', 'seq')), parts along dimension 0, may hold values from -24 to 24
- proj_weight: bfloat16 [3, 4096, 2048], P(None, 'seq', 'head'), may hold values from -1 to 1
- cluster_ids: int32 [16, 4096, 1], P('head', ('groups', 'seq')), parts along dimension 1, may hold values from 0 to 255; in each aligned block of 512 rows (0 to 511, 512 to 1023, ..., all dimensions but the last counted through in order) at most 4 rows name the same one
- centroids: float32 [32, 256, 128], P(('groups', 'head'), 'seq'), parts along dimension 0, may hold values from -3 to 3
Outputs:
- context: bfloat16 [4096, 2048], P(('groups', 'seq'), 'head'), parts along dimension 0
- new_centroids: float32 [32, 256, 128], P(('groups', 'head'), 'seq'), parts along dimension 0
The draws below stay inside these ranges and needn't reach their ends.
There are 2 independent parts, one for each index of `groups`. The reference program is written for one: setup_inputs(seed, part) draws one part's arguments, and reference() takes and returns one part's arrays. A program takes and returns all parts, laid end to end along the dimension named above; an argument that names none is the same for every part. Nothing has to cross between parts.
Inputs may be any that keep to these rules, and one draw needn't show every extreme that they name: `cluster_ids`: for each head, no cluster is named by more than 4 of the 512 tokens of one aligned block (one index of seq); some blocks reach 4.
All inputs are finite; a program needn't handle non-finite values.
Results may differ from the reference program's by a relative error of at most 0.018.
Values may be sent and summed in bfloat16 or wider, within the bound.
A program may use at most 64 MiB of HBM per device.

```python
import math
import jax
import jax.numpy as jnp
import numpy as np
from jax import lax

D = 4096
HEADS = 16
HS = 128
CLUSTERS = 256
TOK_DEV = 512
SLOTS = 4
TOKENS = 2048
N_SEQ = 4


def draw_tokens(key, part):
    values_base = jnp.clip(jax.random.normal(jax.random.fold_in(key, 11), (TOKENS, D), jnp.float32), -4.0, 4.0)
    return values_base.astype(jnp.bfloat16)


def draw_proj_weight(key, part):
    drawn = jnp.clip(jax.random.normal(jax.random.fold_in(key, 21), (3, D, HEADS * HS), jnp.float32), -4.0, 4.0) * D ** (-0.5)
    return drawn.astype(jnp.bfloat16)


def block_levels(rng, shape, cuts, low, high):
    def one(axis_at, blocks):
        heights = jax.random.uniform(jax.random.fold_in(jax.random.fold_in(rng, 6), axis_at), (blocks,), jnp.float32, low / len(cuts), high / len(cuts))
        return jnp.repeat(jnp.exp(heights), shape[axis_at] // blocks).reshape((-1,) + (1,) * (len(shape) - axis_at - 1))

    factor_of = one(*cuts[0])
    for cut in cuts[1:]:
        factor_of = factor_of * one(*cut)
    return factor_of


def routed_block(stream_key, own, number, rows, count, top, reach, skew):
    order = jax.random.permutation(stream_key, count)
    heavy_load, ordinary = load_shares(count, rows * top, reach, skew, True), load_shares(count, rows * top, reach, skew, False)
    places = jnp.arange(count)

    def named(sizes, rotation):
        used = int((sizes > 0).sum())
        fixed = max(1, used // 4)
        shifted = fixed + (places - fixed + rotation * (used - fixed)) % max(1, count - fixed)
        return jnp.zeros((count,), jnp.int32).at[order[jnp.where(places < fixed, places, shifted)]].set(jnp.asarray(sizes, jnp.int32))

    sizes = jnp.where(number % 4 == 0, named(heavy_load, number // 4), named(ordinary, number - number // 4 - 1))
    mixed = jax.random.permutation(jax.random.fold_in(own, 3), count)
    donor, taker = mixed[0:count // 2 * 2:2], mixed[1:count // 2 * 2:2]
    room = jnp.minimum(sizes[donor] - 1, reach - sizes[taker]) // 2
    room = jnp.where((donor == order[0]) | (taker == order[0]) | (sizes[taker] == 0), 0, jnp.maximum(room, 0))
    shifted = jax.random.randint(jax.random.fold_in(own, 4), (count // 2,), 0, 1 << 20) % (room + 1)
    sizes = sizes.at[donor].add(-shifted).at[taker].add(shifted)
    items = jnp.searchsorted(jnp.cumsum(sizes), jnp.arange(rows * top), side="right").astype(jnp.int32)
    grid = items.reshape(top, rows).T
    grid = grid[jax.random.permutation(jax.random.fold_in(own, 1), rows)]
    rotation = jax.random.randint(jax.random.fold_in(own, 2), (rows, 1), 0, top)
    return jnp.take_along_axis(grid, (jnp.arange(top)[None, :] + rotation) % top, axis=1)


def load_shares(number_of, total, most, lean, full):
    weights = [(1 << 20) // math.isqrt(rank ** lean) + 1 for rank in range(1, number_of + 1)]
    largest = most if full else min(most, max(-(-total // number_of), total * weights[0] // sum(weights)))
    least = 1 if total - largest >= number_of - 1 else 0
    given, surplus = [largest] + [least] * (number_of - 1), total - largest - least * (number_of - 1)
    while surplus > 0:
        movable = [i for i in range(1, number_of) if given[i] < largest] or [i for i in range(1, number_of) if given[i] < most]
        mass, remaining = sum([weights[i] for i in movable]), surplus
        for i in movable:
            addition = min(most - given[i], max(1, remaining * weights[i] // mass), surplus)
            given[i] = given[i] + addition
            surplus = surplus - addition
    return np.array(given)


def centred(key, dims, width, bound, shards=(), held_as=jnp.bfloat16):
    result = width * jax.random.normal(key, dims, jnp.float32)
    if shards:
        result = result * block_levels(key, dims, shards, -0.22, 0.18)
    return jnp.clip(result, -bound, bound).astype(held_as)


def setup_inputs(seed: int = 0, part: int = 0) -> dict:
    key_list = jax.random.split(jax.random.key(seed), 5)
    part_splits = jax.random.split(jax.random.fold_in(key_list[4], part), 5)
    tokens = draw_tokens(jax.random.fold_in(jax.random.fold_in(key_list[4], part), 71), part)
    proj_weight = draw_proj_weight(jax.random.fold_in(key_list[4], 71), part)
    cluster_ids_keys = jax.random.split(jax.random.fold_in(part_splits[2], 1), HEADS * TOKENS // TOK_DEV)
    cluster_ids_turns = jax.random.permutation(jax.random.fold_in(part_splits[2], 3), HEADS * TOKENS // TOK_DEV)
    cluster_ids = jax.vmap(lambda own, number: routed_block(jax.random.fold_in(part_splits[2], 2), own, number, TOK_DEV, CLUSTERS, 1, SLOTS, 2))(cluster_ids_keys, cluster_ids_turns).reshape((HEADS, TOKENS, 1))
    centroids = centred(part_splits[3], (HEADS, CLUSTERS, HS), 0.5, 3.0, ((0, 4), (1, 4)), jnp.float32)
    return {"tokens": tokens, "proj_weight": proj_weight, "cluster_ids": cluster_ids, "centroids": centroids}


def one_head(inputs):
    queries, key_rows, value_rows, member, current = inputs
    capacity = N_SEQ * SLOTS
    labels = jnp.arange(CLUSTERS, dtype=jnp.int32)
    onehot = (member[:, None] == labels[None, :]).astype(jnp.int32)
    blocks = onehot.reshape(N_SEQ, TOK_DEV, CLUSTERS)
    prior = (jnp.cumsum(blocks, axis=1) - blocks).reshape(TOKENS, CLUSTERS).astype(jnp.int32)
    ranking = jnp.sum(prior * onehot, axis=1).astype(jnp.int32)
    source = jnp.arange(TOKENS, dtype=jnp.int32) // TOK_DEV
    slot_index = (source * SLOTS + ranking).astype(jnp.int32)
    packed = jnp.concatenate([queries, key_rows, value_rows], axis=1)
    outbox = jnp.zeros((CLUSTERS, capacity, 3 * HS), jnp.bfloat16).at[member, slot_index].set(packed)
    filled = jnp.zeros((CLUSTERS, capacity), jnp.int32).at[member, slot_index].set(1)
    query_block = outbox[:, :, :HS].astype(jnp.float32)
    key_block = outbox[:, :, HS:2 * HS].astype(jnp.float32)
    value_block = outbox[:, :, 2 * HS:].astype(jnp.float32)
    scores = jnp.einsum("cqd,ckd->cqk", query_block, key_block, precision=lax.Precision.HIGHEST) * (HS ** -0.5)
    ordinal = jnp.arange(capacity, dtype=jnp.int32)
    allowed = ((filled[:, None, :] > 0) & (ordinal[None, None, :] <= ordinal[None, :, None])) | (ordinal[None, None, :] == ordinal[None, :, None])
    scores = jnp.where(allowed, scores, -1e30)
    row_max = jnp.max(scores, axis=2, keepdims=True)
    raised = jnp.exp(scores - row_max)
    weights = (raised / jnp.sum(raised, axis=2, keepdims=True)).astype(jnp.bfloat16)
    attended = jnp.einsum("cqk,ckd->cqd", weights.astype(jnp.float32), value_block, precision=lax.Precision.HIGHEST).astype(jnp.bfloat16)
    context = attended[member, slot_index]
    key_sums = jnp.dot(onehot.astype(jnp.float32).T, key_rows.astype(jnp.float32), precision=lax.Precision.HIGHEST)
    counts = jnp.sum(onehot, axis=0).astype(jnp.float32)
    updated = 0.25 * current + 0.75 * key_sums / jnp.maximum(counts, 1.0)[:, None]
    return context, updated


def reference(tokens, proj_weight, cluster_ids, centroids):
    stacked = []
    for which in range(3):
        projected = jnp.dot(tokens, proj_weight[which], preferred_element_type=jnp.float32).astype(jnp.bfloat16)
        stacked.append(projected.reshape(TOKENS, HEADS, HS).transpose(1, 0, 2))
    contexts, updated = lax.map(one_head, (stacked[0], stacked[1], stacked[2], cluster_ids[:, :, 0], centroids))
    context = contexts.transpose(1, 0, 2).reshape(TOKENS, HEADS * HS)
    return context, updated
```

```python
import functools

import jax
import jax.numpy as jnp
from jax import lax
from jax.experimental import pallas as pl
from jax.experimental.pallas import tpu as pltpu
from jax.sharding import PartitionSpec as P

HS = 128
CLUSTERS = 256
SLOTS = 4


def general(tokens, proj_weight, cluster_ids, centroids):
    owners = lax.axis_size("seq")
    local_rows = tokens.shape[0]
    columns = proj_weight.shape[2]
    head_count = columns // HS
    owned = CLUSTERS // owners
    capacity = owners * SLOTS
    score_scale = HS ** (-0.5)
    projected = jnp.einsum(
        "td,pdc->ptc",
        tokens,
        lax.all_gather(proj_weight, "seq", axis=1, tiled=True),
        preferred_element_type=jnp.float32,
    ).astype(jnp.bfloat16)
    per_head = projected.reshape(3, local_rows, head_count, HS).transpose(2, 1, 0, 3)
    packed = per_head.reshape(head_count, local_rows, 3 * HS)
    member = cluster_ids[:, :, 0]
    labels = jnp.arange(CLUSTERS, dtype=jnp.int32)
    onehot = (member[:, :, None] == labels[None, None, :]).astype(jnp.bfloat16)
    ordinal_rows = jnp.arange(local_rows, dtype=jnp.int32)
    earlier = (ordinal_rows[None, :] < ordinal_rows[:, None]).astype(jnp.bfloat16)
    before = jnp.einsum("ts,hsc->htc", earlier, onehot, preferred_element_type=jnp.float32)
    ranking = jnp.take_along_axis(before, member[:, :, None], axis=2)[:, :, 0].astype(jnp.int32)
    placed = member * SLOTS + ranking
    head_index = jnp.arange(head_count, dtype=jnp.int32)[:, None]
    outbox = (
        jnp.zeros((head_count, CLUSTERS * SLOTS, 3 * HS), jnp.bfloat16)
        .at[head_index, placed]
        .set(packed)
    )
    outbox = outbox.reshape(head_count, owners, owned * SLOTS, 3 * HS)
    local_counts = jnp.sum(onehot, axis=1, dtype=jnp.float32)
    tallies = local_counts.astype(jnp.int32).reshape(head_count, owners, owned)
    blocks = lax.all_to_all(outbox, "seq", split_axis=1, concat_axis=1, tiled=True)
    arrived = lax.all_to_all(tallies, "seq", split_axis=1, concat_axis=1, tiled=True)
    local_heads = blocks.shape[0]
    arranged = (
        blocks.reshape(local_heads, owners, owned, SLOTS, 3 * HS)
        .transpose(0, 2, 1, 3, 4)
        .reshape(local_heads, owned, capacity, 3 * HS)
    )
    filled = jnp.arange(SLOTS, dtype=jnp.int32)[None, None, None, :] < arrived[:, :, :, None]
    filled = filled.transpose(0, 2, 1, 3).reshape(local_heads, owned, capacity)
    queries = arranged[:, :, :, :HS]
    key_block = arranged[:, :, :, HS : 2 * HS]
    value_block = arranged[:, :, :, 2 * HS :]
    scores = (
        jnp.einsum("hcqd,hckd->hcqk", queries, key_block, preferred_element_type=jnp.float32)
        * score_scale
    )
    ordinal = jnp.arange(capacity, dtype=jnp.int32)
    causal = ordinal[None, None, None, :] <= ordinal[None, None, :, None]
    itself = ordinal[None, None, None, :] == ordinal[None, None, :, None]
    allowed = filled[:, :, None, :] & causal | itself
    scores = jnp.where(allowed, scores, -1e30)
    row_max = jnp.max(scores, axis=3, keepdims=True)
    raised = jnp.exp(scores - row_max)
    weights = (raised / jnp.sum(raised, axis=3, keepdims=True)).astype(jnp.bfloat16)
    attended = jnp.einsum(
        "hcqk,hckd->hcqd", weights, value_block, preferred_element_type=jnp.float32
    ).astype(jnp.bfloat16)
    attended = (
        attended.reshape(local_heads, owned, owners, SLOTS, HS)
        .transpose(0, 2, 1, 3, 4)
        .reshape(local_heads, owners, owned * SLOTS, HS)
    )
    returned = lax.all_to_all(attended, "seq", split_axis=1, concat_axis=1, tiled=True)
    key_sums = jnp.einsum(
        "hck,hckd->hcd", filled.astype(jnp.bfloat16), key_block, preferred_element_type=jnp.float32
    )
    counts = jnp.sum(filled, axis=2).astype(jnp.float32)
    exchanged = (returned, key_sums, counts)
    returned, key_sums, counts = exchanged
    gathered = returned.reshape(head_count, CLUSTERS * SLOTS, HS)
    mine = jax.vmap(lambda table, where: table[where])(gathered, placed)
    context = mine.transpose(1, 0, 2).reshape(local_rows, head_count * HS)
    updated = 0.25 * centroids + 0.75 * key_sums / jnp.maximum(counts, 1.0)[:, :, None]
    return (context, updated)


MESH = pl.DeviceIdType.MESH
PIECES = 4
ROWS = 256
QROWS = 128


def kernel(
    tok_hbm, w_hbm, ids_hbm, cent_ref, ctx_ref, new_ref,
    tok, w, qkv, ids, ids_col, ctx_out, cent_out, cent_in,
    local_sem, ids_send, ids_recv, wz_send, wz_recv, wy_send, wy_recv,
    z_send, z_recv, x_send, x_recv, c_send, c_recv, ctx_send, ctx_recv, cent_send, cent_recv,
):
    g = lax.axis_index("groups")
    z = lax.axis_index("seq")
    h = lax.axis_index("head")
    n = lax.axis_size("seq")
    block = tok_hbm.shape[0]
    depth = w_hbm.shape[1]
    half = depth // 2
    piece = block // PIECES // 4
    group = block // PIECES
    quarter = h
    over_x = (g, z, lax.rem(h + 2, 4))
    over_c = (g, z, h + 1 - 2 * lax.rem(h, 2))
    over_y = (1 - g, z, h)

    barrier = pltpu.get_barrier_semaphore()
    for d in range(1, n):
        pl.semaphore_signal(barrier, inc=1, device_id=(g, lax.rem(z + d, n), h), device_id_type=MESH)
    for peer in (over_x, over_c, over_y):
        pl.semaphore_signal(barrier, inc=1, device_id=peer, device_id_type=MESH)
    pl.semaphore_wait(barrier, n + 2)

    def remote(src, dst, send, recv, device):
        return pltpu.make_async_remote_copy(
            src_ref=src, dst_ref=dst, send_sem=send, recv_sem=recv, device_id=device, device_id_type=MESH
        )

    def col(j):
        return pl.ds(pl.multiple_of(j * HS, HS), HS)

    def rows_of(src, p, q):
        return pl.ds(pl.multiple_of(src * block + p * group + q * piece, piece), piece)

    def w_copy(d, j):
        to = lax.rem(z + d, n)
        return remote(
            w_hbm.at[j, pl.ds(pl.multiple_of(g * half, half), half), col(to)],
            w.at[pl.ds(pl.multiple_of(z * depth + g * half, half), half), pl.ds(j * HS, HS)],
            wz_send.at[d - 1, j], wz_recv.at[d - 1, j], (g, to, h),
        )

    def w_arrived(d, j):
        src = lax.rem(z - d + n, n)
        part = w.at[pl.ds(pl.multiple_of(src * depth + g * half, half), half), pl.ds(j * HS, HS)]
        return part

    def ids_copy(d):
        to = lax.rem(z + d, n)
        return remote(
            ids_hbm.at[to], ids.at[:, pl.ds(pl.multiple_of(z * block, block), block)],
            ids_send.at[d - 1], ids_recv.at[d - 1], (g, to, h),
        )

    for j in range(3):
        for d in range(1, n):
            w_copy(d, j).start()
    for d in range(1, n):
        ids_copy(d).start()

    def own_copy(p, up):
        to = z + 1 if up else z - 1
        return remote(
            tok_hbm.at[pl.ds(pl.multiple_of(p * group + quarter * piece, piece), piece), :],
            tok.at[rows_of(z, p, quarter), :],
            z_send.at[1 if up else 0, z, p], z_recv.at[z, p], (g, to, h),
        )

    @pl.when(z < n - 1)
    def _():
        for p in range(PIECES):
            own_copy(p, True).start()

    @pl.when(z > 0)
    def _():
        for p in range(PIECES):
            own_copy(p, False).start()

    locals_ = [
        pltpu.make_async_copy(tok_hbm, tok.at[pl.ds(pl.multiple_of(z * block, block), block), :], local_sem.at[0]),
        pltpu.make_async_copy(ids_hbm.at[z], ids.at[:, pl.ds(pl.multiple_of(z * block, block), block)], local_sem.at[1]),
    ]
    for j in range(3):
        locals_.append(
            pltpu.make_async_copy(
                w_hbm.at[j, :, col(z)],
                w.at[pl.ds(pl.multiple_of(z * depth, depth), depth), pl.ds(j * HS, HS)],
                local_sem.at[2 + j],
            )
        )
    for copy in locals_:
        copy.start()

    def w_forward(d, j):
        part = w_arrived(d, j)
        return remote(part, part, wy_send.at[d - 1, j], wy_recv.at[d - 1, j], over_y)

    for j in range(3):
        for d in range(1, n):
            w_copy(d, j).wait_recv()
            w_forward(d, j).start()

    def project(start):
        rows = pl.ds(pl.multiple_of(start, ROWS), ROWS)
        qkv[rows, :] = jnp.dot(tok[rows, :], w[...], preferred_element_type=jnp.float32).astype(jnp.bfloat16)

    def source(s):
        low = s + (s >= z).astype(jnp.int32)
        high = n - 1 - (s + (s >= n - 1 - z).astype(jnp.int32))
        return jnp.where(z < n // 2, low, high)

    def split(t):
        return source(t // PIECES), lax.rem(t, PIECES)

    def along(src, p):
        up = (src < z).astype(jnp.int32)
        part = tok.at[rows_of(src, p, quarter), :]
        return remote(part, part, z_send.at[up, src, p], z_recv.at[src, p], (g, z + 2 * up - 1, h))

    def along_exists(src):
        return jnp.where(src < z, z < n - 1, z > 0)

    def across(src, p, q):
        part = tok.at[rows_of(src, p, q), :]
        return remote(part, part, x_send.at[src, p], x_recv.at[src, p], over_x)

    def beside(src, p, which, q):
        part = tok.at[rows_of(src, p, q), :]
        return remote(part, part, c_send.at[which, src, p], c_recv.at[which, src, p], over_c)

    other_x = lax.rem(h + 2, 4)
    sib = h + 1 - 2 * lax.rem(h, 2)
    sib_x = lax.rem(sib + 2, 4)
    steps = (n - 1) * PIECES

    def step(t, carry):
        @pl.when(t < steps)
        def _():
            src, p = split(t)
            along(src, p).wait_recv()

            @pl.when(along_exists(src))
            def _():
                along(src, p).start()

            across(src, p, quarter).start()
            beside(src, p, 0, quarter).start()

        @pl.when((t >= 1) & (t < steps + 1))
        def _():
            src, p = split(t - 1)
            across(src, p, other_x).wait_recv()
            beside(src, p, 1, other_x).start()

        @pl.when(t >= 2)
        def _():
            src, p = split(t - 2)
            beside(src, p, 0, sib).wait_recv()
            beside(src, p, 1, sib_x).wait_recv()

            @pl.when(lax.rem((p + 1) * group, ROWS) == 0)
            def _():
                project(src * block + (p + 1) * group - ROWS)

        return carry

    for j in range(3):
        for d in range(1, n):
            src = lax.rem(z - d + n, n)
            part = w.at[pl.ds(pl.multiple_of(src * depth + (1 - g) * half, half), half), pl.ds(j * HS, HS)]
            remote(part, part, wy_send.at[d - 1, j], wy_recv.at[d - 1, j], over_y).wait_recv()
    for copy in locals_:
        copy.wait()

    def own_rows(i, carry):
        project(z * block + i * ROWS)
        return carry

    lax.fori_loop(0, block // ROWS, own_rows, 0)
    lax.fori_loop(0, steps + 2, step, 0)

    for d in range(1, n):
        ids_copy(d).wait_recv()
    total = n * block
    for i in range(total // 128):
        row = ids[0:1, i * 128 : (i + 1) * 128].astype(jnp.float32)
        ids_col[i * 128 : (i + 1) * 128, :] = jnp.broadcast_to(row, (128, 128)).T
    scale = HS ** (-0.5)

    def context_copy(i):
        return remote(
            ctx_out.at[pl.ds(i * block, block), :], ctx_ref.at[:, col(z)],
            ctx_send.at[i], ctx_recv.at[z], (g, i, h),
        )

    def attend(i):
        length = (i + 1) * block
        key_ids = ids[0:1, 0:length].astype(jnp.float32)

        def body(b, carry):
            start = pl.multiple_of(i * block + b * QROWS, QROWS)
            rows = pl.ds(start, QROWS)
            scores = lax.dot_general(
                qkv[rows, 0:HS], qkv[0:length, HS : 2 * HS], (((1,), (1,)), ((), ())),
                preferred_element_type=jnp.float32,
            ) * scale
            at_query = start + lax.broadcasted_iota(jnp.int32, (QROWS, length), 0)
            at_key = lax.broadcasted_iota(jnp.int32, (QROWS, length), 1)
            allowed = (ids_col[rows, 0:1] == key_ids) & (at_key <= at_query)
            scores = jnp.where(allowed, scores, -1e30)
            raised = jnp.exp(scores - jnp.max(scores, axis=1, keepdims=True))
            inverse = 1.0 / jnp.sum(raised, axis=1, keepdims=True)
            weights = (raised * inverse).astype(jnp.bfloat16)
            ctx_out[rows, :] = jnp.dot(
                weights, qkv[0:length, 2 * HS : 3 * HS], preferred_element_type=jnp.float32
            ).astype(jnp.bfloat16)
            return carry

        lax.fori_loop(0, block // QROWS, body, 0)

        @pl.when(i != z)
        def _():
            context_copy(i).start()

    clusters = cent_in.shape[1] * n
    owned = cent_in.shape[1]
    labels = lax.broadcasted_iota(jnp.int32, (clusters, total), 0)
    member = (labels == ids[0:1, :]).astype(jnp.float32)
    counts = jnp.sum(member, axis=1, keepdims=True)
    key_sums = jnp.dot(
        member.astype(jnp.bfloat16), qkv[:, HS : 2 * HS], preferred_element_type=jnp.float32
    )
    share = 0.75 * key_sums / jnp.maximum(counts, 1.0)
    for i in range(n):
        cent_out[i] = share[i * owned : (i + 1) * owned, :]

    def cent_copy(i):
        return remote(cent_out.at[i], cent_in.at[z], cent_send.at[i], cent_recv.at[z], (g, i, h))

    for i in range(n):
        @pl.when(i != z)
        def _():
            cent_copy(i).start()

    for i in range(n):
        attend(i)

    ctx_ref[:, col(z)] = ctx_out[pl.ds(pl.multiple_of(z * block, block), block), :]
    cent_in[z] = cent_out[z]

    for i in range(n):
        @pl.when(i != z)
        def _():
            remote(cent_out.at[i], cent_in.at[i], cent_send.at[i], cent_recv.at[i], (g, i, h)).wait_recv()
    new_ref[...] = 0.25 * cent_ref[...] + cent_in[...]

    for j in range(3):
        for d in range(1, n):
            w_copy(d, j).wait_send()
            w_forward(d, j).wait_send()
    for d in range(1, n):
        ids_copy(d).wait_send()

    @pl.when(z < n - 1)
    def _():
        for p in range(PIECES):
            own_copy(p, True).wait_send()

    @pl.when(z > 0)
    def _():
        for p in range(PIECES):
            own_copy(p, False).wait_send()

    def drain(t, carry):
        src, p = split(t)

        @pl.when(along_exists(src))
        def _():
            along(src, p).wait_send()

        across(src, p, quarter).wait_send()
        beside(src, p, 0, quarter).wait_send()
        beside(src, p, 1, other_x).wait_send()
        return carry

    lax.fori_loop(0, steps, drain, 0)
    for i in range(n):
        @pl.when(i != z)
        def _():
            cent_copy(i).wait_send()
            context_copy(i).wait_send()
            remote(
                ctx_out.at[pl.ds(i * block, block), :], ctx_ref.at[:, pl.ds(i * HS, HS)],
                ctx_send.at[i], ctx_recv.at[i], (g, i, h),
            ).wait_recv()


def by_head(tokens, proj_weight, cluster_ids, centroids):
    n = lax.axis_size("seq")
    block, width = tokens.shape
    heads = cluster_ids.shape[0]
    owned = centroids.shape[1]
    ids = jnp.broadcast_to(cluster_ids.reshape(heads, 1, block), (heads, 8, block))
    dma = pltpu.SemaphoreType.DMA
    return tuple(
        pl.pallas_call(
            kernel,
            out_shape=(
                jax.ShapeDtypeStruct((block, heads * HS), jnp.bfloat16),
                jax.ShapeDtypeStruct((heads, owned, HS), jnp.float32),
            ),
            in_specs=[pl.BlockSpec(memory_space=pl.ANY)] * 3 + [pl.BlockSpec(memory_space=pltpu.VMEM)],
            out_specs=(pl.BlockSpec(memory_space=pltpu.VMEM), pl.BlockSpec(memory_space=pltpu.VMEM)),
            scratch_shapes=[
                pltpu.VMEM((n * block, width), jnp.bfloat16),
                pltpu.VMEM((width, 3 * HS), jnp.bfloat16),
                pltpu.VMEM((n * block, 3 * HS), jnp.bfloat16),
                pltpu.VMEM((8, n * block), jnp.int32),
                pltpu.VMEM((n * block, HS), jnp.float32),
                pltpu.VMEM((n * block, HS), jnp.bfloat16),
                pltpu.VMEM((n, owned, HS), jnp.float32),
                pltpu.VMEM((n, owned, HS), jnp.float32),
                dma((5,)),
                dma((n - 1,)), dma((n - 1,)),
                dma((n - 1, 3)), dma((n - 1, 3)),
                dma((n - 1, 3)), dma((n - 1, 3)),
                dma((2, n, PIECES)), dma((n, PIECES)),
                dma((n, PIECES)), dma((n, PIECES)),
                dma((2, n, PIECES)), dma((2, n, PIECES)),
                dma((n,)), dma((n,)),
                dma((n,)), dma((n,)),
            ],
            compiler_params=pltpu.CompilerParams(
                collective_id=0, has_side_effects=True, vmem_limit_bytes=58 << 20
            ),
        )(tokens, proj_weight, ids, centroids)
    )


def local(tokens, proj_weight, cluster_ids, centroids):
    heads = cluster_ids.shape[0]
    fits = (
        lax.axis_size("seq") == heads
        and lax.axis_size("head") == 4
        and lax.axis_size("groups") == 2
        and tokens.shape[0] % ROWS == 0
    )
    return (by_head if fits else general)(tokens, proj_weight, cluster_ids, centroids)


def solution(mesh):
    return jax.shard_map(
        local,
        mesh=mesh,
        in_specs=(
            P(("groups", "seq"), None),
            P(None, "seq", "head"),
            P("head", ("groups", "seq"), None),
            P(("groups", "head"), "seq", None),
        ),
        out_specs=(P(("groups", "seq"), "head"), P(("groups", "head"), "seq", None)),
        check_vma=False,
    )
```

```python
import functools

import jax
import jax.numpy as jnp
from jax import lax
from jax.experimental import pallas as pl
from jax.experimental.pallas import tpu as pltpu
from jax.sharding import PartitionSpec as P

HS = 128
CLUSTERS = 256
SLOTS = 4


def general(tokens, proj_weight, cluster_ids, centroids):
    owners = lax.axis_size("seq")
    local_rows = tokens.shape[0]
    columns = proj_weight.shape[2]
    head_count = columns // HS
    owned = CLUSTERS // owners
    capacity = owners * SLOTS
    score_scale = HS ** (-0.5)
    projected = jnp.einsum(
        "td,pdc->ptc",
        tokens,
        lax.all_gather(proj_weight, "seq", axis=1, tiled=True),
        preferred_element_type=jnp.float32,
    ).astype(jnp.bfloat16)
    per_head = projected.reshape(3, local_rows, head_count, HS).transpose(2, 1, 0, 3)
    packed = per_head.reshape(head_count, local_rows, 3 * HS)
    member = cluster_ids[:, :, 0]
    labels = jnp.arange(CLUSTERS, dtype=jnp.int32)
    onehot = (member[:, :, None] == labels[None, None, :]).astype(jnp.bfloat16)
    ordinal_rows = jnp.arange(local_rows, dtype=jnp.int32)
    earlier = (ordinal_rows[None, :] < ordinal_rows[:, None]).astype(jnp.bfloat16)
    before = jnp.einsum("ts,hsc->htc", earlier, onehot, preferred_element_type=jnp.float32)
    ranking = jnp.take_along_axis(before, member[:, :, None], axis=2)[:, :, 0].astype(jnp.int32)
    placed = member * SLOTS + ranking
    head_index = jnp.arange(head_count, dtype=jnp.int32)[:, None]
    outbox = (
        jnp.zeros((head_count, CLUSTERS * SLOTS, 3 * HS), jnp.bfloat16)
        .at[head_index, placed]
        .set(packed)
    )
    outbox = outbox.reshape(head_count, owners, owned * SLOTS, 3 * HS)
    local_counts = jnp.sum(onehot, axis=1, dtype=jnp.float32)
    tallies = local_counts.astype(jnp.int32).reshape(head_count, owners, owned)
    blocks = lax.all_to_all(outbox, "seq", split_axis=1, concat_axis=1, tiled=True)
    arrived = lax.all_to_all(tallies, "seq", split_axis=1, concat_axis=1, tiled=True)
    local_heads = blocks.shape[0]
    arranged = (
        blocks.reshape(local_heads, owners, owned, SLOTS, 3 * HS)
        .transpose(0, 2, 1, 3, 4)
        .reshape(local_heads, owned, capacity, 3 * HS)
    )
    filled = jnp.arange(SLOTS, dtype=jnp.int32)[None, None, None, :] < arrived[:, :, :, None]
    filled = filled.transpose(0, 2, 1, 3).reshape(local_heads, owned, capacity)
    queries = arranged[:, :, :, :HS]
    key_block = arranged[:, :, :, HS : 2 * HS]
    value_block = arranged[:, :, :, 2 * HS :]
    scores = (
        jnp.einsum("hcqd,hckd->hcqk", queries, key_block, preferred_element_type=jnp.float32)
        * score_scale
    )
    ordinal = jnp.arange(capacity, dtype=jnp.int32)
    causal = ordinal[None, None, None, :] <= ordinal[None, None, :, None]
    itself = ordinal[None, None, None, :] == ordinal[None, None, :, None]
    allowed = filled[:, :, None, :] & causal | itself
    scores = jnp.where(allowed, scores, -1e30)
    row_max = jnp.max(scores, axis=3, keepdims=True)
    raised = jnp.exp(scores - row_max)
    weights = (raised / jnp.sum(raised, axis=3, keepdims=True)).astype(jnp.bfloat16)
    attended = jnp.einsum(
        "hcqk,hckd->hcqd", weights, value_block, preferred_element_type=jnp.float32
    ).astype(jnp.bfloat16)
    attended = (
        attended.reshape(local_heads, owned, owners, SLOTS, HS)
        .transpose(0, 2, 1, 3, 4)
        .reshape(local_heads, owners, owned * SLOTS, HS)
    )
    returned = lax.all_to_all(attended, "seq", split_axis=1, concat_axis=1, tiled=True)
    key_sums = jnp.einsum(
        "hck,hckd->hcd", filled.astype(jnp.bfloat16), key_block, preferred_element_type=jnp.float32
    )
    counts = jnp.sum(filled, axis=2).astype(jnp.float32)
    exchanged = (returned, key_sums, counts)
    returned, key_sums, counts = exchanged
    gathered = returned.reshape(head_count, CLUSTERS * SLOTS, HS)
    mine = jax.vmap(lambda table, where: table[where])(gathered, placed)
    context = mine.transpose(1, 0, 2).reshape(local_rows, head_count * HS)
    updated = 0.25 * centroids + 0.75 * key_sums / jnp.maximum(counts, 1.0)[:, :, None]
    return (context, updated)


MESH = pl.DeviceIdType.MESH
PIECES = 4
ROWS = 256
QROWS = 128


def kernel(
    tok_hbm, w_hbm, ids_hbm, cent_ref, ctx_ref, new_ref,
    tok, w, qkv, ids, ids_col, member, counts, ctx_out, cent_out, cent_in,
    local_sem, ids_send, ids_recv, wz_send, wz_recv, wy_send, wy_recv,
    z_send, z_recv, x_send, x_recv, c_send, c_recv, ctx_send, ctx_recv, cent_send, cent_recv,
):
    g = lax.axis_index("groups")
    z = lax.axis_index("seq")
    h = lax.axis_index("head")
    n = lax.axis_size("seq")
    block = tok_hbm.shape[0]
    depth = w_hbm.shape[1]
    half = depth // 2
    piece = block // PIECES // 4
    group = block // PIECES
    quarter = h
    over_x = (g, z, lax.rem(h + 2, 4))
    over_c = (g, z, h + 1 - 2 * lax.rem(h, 2))
    over_y = (1 - g, z, h)

    barrier = pltpu.get_barrier_semaphore()
    for d in range(1, n):
        pl.semaphore_signal(barrier, inc=1, device_id=(g, lax.rem(z + d, n), h), device_id_type=MESH)
    for peer in (over_x, over_c, over_y):
        pl.semaphore_signal(barrier, inc=1, device_id=peer, device_id_type=MESH)
    pl.semaphore_wait(barrier, n + 2)

    def remote(src, dst, send, recv, device):
        return pltpu.make_async_remote_copy(
            src_ref=src, dst_ref=dst, send_sem=send, recv_sem=recv, device_id=device, device_id_type=MESH
        )

    def col(j):
        return pl.ds(pl.multiple_of(j * HS, HS), HS)

    def rows_of(src, p, q):
        return pl.ds(pl.multiple_of(src * block + p * group + q * piece, piece), piece)

    def w_copy(d, j):
        to = lax.rem(z + d, n)
        return remote(
            w_hbm.at[j, pl.ds(pl.multiple_of(g * half, half), half), col(to)],
            w.at[pl.ds(pl.multiple_of(z * depth + g * half, half), half), pl.ds(j * HS, HS)],
            wz_send.at[d - 1, j], wz_recv.at[d - 1, j], (g, to, h),
        )

    def w_arrived(d, j):
        src = lax.rem(z - d + n, n)
        part = w.at[pl.ds(pl.multiple_of(src * depth + g * half, half), half), pl.ds(j * HS, HS)]
        return part

    def ids_copy(d):
        to = lax.rem(z + d, n)
        return remote(
            ids_hbm.at[to], ids.at[:, pl.ds(pl.multiple_of(z * block, block), block)],
            ids_send.at[d - 1], ids_recv.at[d - 1], (g, to, h),
        )

    for d in range(1, n):
        ids_copy(d).start()

    def own_copy(p, up):
        to = z + 1 if up else z - 1
        return remote(
            tok_hbm.at[pl.ds(pl.multiple_of(p * group + quarter * piece, piece), piece), :],
            tok.at[rows_of(z, p, quarter), :],
            z_send.at[1 if up else 0, z, p], z_recv.at[z, p], (g, to, h),
        )

    def own_start(up):
        for p in range(PIECES):
            own_copy(p, up).start()

    pl.when(z == 1)(lambda: own_start(False))
    pl.when(z == n - 2)(lambda: own_start(True))
    for j in range(3):
        for d in range(1, n):
            w_copy(d, j).start()
    pl.when((z != 1) & (z < n - 2))(lambda: own_start(True))
    pl.when(z > 1)(lambda: own_start(False))

    locals_ = [
        pltpu.make_async_copy(tok_hbm, tok.at[pl.ds(pl.multiple_of(z * block, block), block), :], local_sem.at[0]),
        pltpu.make_async_copy(ids_hbm.at[z], ids.at[:, pl.ds(pl.multiple_of(z * block, block), block)], local_sem.at[1]),
    ]
    for j in range(3):
        locals_.append(
            pltpu.make_async_copy(
                w_hbm.at[j, :, col(z)],
                w.at[pl.ds(pl.multiple_of(z * depth, depth), depth), pl.ds(j * HS, HS)],
                local_sem.at[2 + j],
            )
        )
    for copy in locals_:
        copy.start()

    def w_forward(d, j):
        part = w_arrived(d, j)
        return remote(part, part, wy_send.at[d - 1, j], wy_recv.at[d - 1, j], over_y)

    def w_step(j):
        for d in range(1, n):
            w_copy(d, j).wait_recv()
            w_forward(d, j).start()

    def project(start):
        rows = pl.ds(pl.multiple_of(start, ROWS), ROWS)
        qkv[rows, :] = jnp.dot(tok[rows, :], w[...], preferred_element_type=jnp.float32).astype(jnp.bfloat16)

    def source(s):
        low = s + (s >= z).astype(jnp.int32)
        high = jnp.where(s == 0, 2 * n - 3 - z, s - 1)
        return jnp.where(z < n // 2, low, high)

    def split(t):
        return source(t // PIECES), lax.rem(t, PIECES)

    def along(src, p):
        up = (src < z).astype(jnp.int32)
        part = tok.at[rows_of(src, p, quarter), :]
        return remote(part, part, z_send.at[up, src, p], z_recv.at[src, p], (g, z + 2 * up - 1, h))

    def along_exists(src):
        return jnp.where(src < z, z < n - 1, z > 0)

    def across(src, p, q):
        part = tok.at[rows_of(src, p, q), :]
        return remote(part, part, x_send.at[src, p], x_recv.at[src, p], over_x)

    def beside(src, p, which, q):
        part = tok.at[rows_of(src, p, q), :]
        return remote(part, part, c_send.at[which, src, p], c_recv.at[which, src, p], over_c)

    other_x = lax.rem(h + 2, 4)
    sib = h + 1 - 2 * lax.rem(h, 2)
    sib_x = lax.rem(sib + 2, 4)
    steps = (n - 1) * PIECES

    inner = (z > 0) & (z < n - 1)

    def carry_on(t):
        src, p = split(t)
        along(src, p).wait_recv()

        @pl.when(along_exists(src))
        def _():
            along(src, p).start()

        across(src, p, quarter).start()
        beside(src, p, 0, quarter).start()

    def hand_over(t):
        src, p = split(t)
        across(src, p, other_x).wait_recv()
        beside(src, p, 1, other_x).start()

    def complete(t):
        src, p = split(t)
        beside(src, p, 0, sib).wait_recv()
        beside(src, p, 1, sib_x).wait_recv()
        return src, p

    for d in range(1, n):
        ids_copy(d).wait_recv()
    for copy in locals_[:2]:
        copy.wait()
    total = n * block
    for i in range(total // 128):
        row = ids[0:1, i * 128 : (i + 1) * 128].astype(jnp.float32)
        ids_col[i * 128 : (i + 1) * 128, :] = jnp.broadcast_to(row, (128, 128)).T
    owned = cent_in.shape[1]
    clusters = owned * n
    labels = lax.broadcasted_iota(jnp.int32, (clusters, total), 0)
    named = (labels == ids[0:1, :]).astype(jnp.float32)
    counts[...] = jnp.broadcast_to(jnp.sum(named, axis=1, keepdims=True), counts.shape)
    member[...] = named.astype(jnp.bfloat16)

    for t in range(PIECES):
        if t < 3:
            pl.when(inner)(lambda: w_step(t))
        carry_on(t)
        if t < 3:
            pl.when(~inner)(lambda: w_step(t))
        if t >= 1:
            hand_over(t - 1)
        if t >= 2:
            complete(t - 2)

    pl.when(z == 1)(lambda: own_start(True))

    def rest(t, carry):
        pl.when(t < steps)(lambda: carry_on(t))
        pl.when(t < steps + 1)(lambda: hand_over(t - 1))
        src, p = complete(t - 2)

        @pl.when((t >= PIECES + 2) & (lax.rem((p + 1) * group, ROWS) == 0))
        def _():
            project(src * block + (p + 1) * group - ROWS)

        return carry

    lax.fori_loop(PIECES, PIECES + 2, rest, 0)

    for j in range(3):
        for d in range(1, n):
            src = lax.rem(z - d + n, n)
            part = w.at[pl.ds(pl.multiple_of(src * depth + (1 - g) * half, half), half), pl.ds(j * HS, HS)]
            remote(part, part, wy_send.at[d - 1, j], wy_recv.at[d - 1, j], over_y).wait_recv()
    for copy in locals_[2:]:
        copy.wait()

    def early_rows(i, carry):
        which = jnp.where(i < block // ROWS, z, source(0))
        project(which * block + lax.rem(i, block // ROWS) * ROWS)
        return carry

    lax.fori_loop(0, 2 * (block // ROWS), early_rows, 0)
    scale = HS ** (-0.5)

    def context_copy(i):
        return remote(
            ctx_out.at[pl.ds(i * block, block), :], ctx_ref.at[:, col(z)],
            ctx_send.at[i], ctx_recv.at[z], (g, i, h),
        )

    def attend(i):
        length = (i + 1) * block
        key_ids = ids[0:1, 0:length].astype(jnp.float32)

        def body(b, carry):
            start = pl.multiple_of(i * block + b * QROWS, QROWS)
            rows = pl.ds(start, QROWS)
            scores = lax.dot_general(
                qkv[rows, 0:HS], qkv[0:length, HS : 2 * HS], (((1,), (1,)), ((), ())),
                preferred_element_type=jnp.float32,
            ) * scale
            at_query = start + lax.broadcasted_iota(jnp.int32, (QROWS, length), 0)
            at_key = lax.broadcasted_iota(jnp.int32, (QROWS, length), 1)
            allowed = (ids_col[rows, 0:1] == key_ids) & (at_key <= at_query)
            scores = jnp.where(allowed, scores, -1e30)
            raised = jnp.exp(scores - jnp.max(scores, axis=1, keepdims=True))
            inverse = 1.0 / jnp.sum(raised, axis=1, keepdims=True)
            weights = (raised * inverse).astype(jnp.bfloat16)
            ctx_out[rows, :] = jnp.dot(
                weights, qkv[0:length, 2 * HS : 3 * HS], preferred_element_type=jnp.float32
            ).astype(jnp.bfloat16)
            return carry

        lax.fori_loop(0, block // QROWS, body, 0)

        @pl.when(i != z)
        def _():
            context_copy(i).start()

    lax.fori_loop(PIECES + 2, 2 * PIECES + 2, rest, 0)
    attend(0)

    @pl.when(z < n // 2)
    def _():
        for i in range(1, n - 1):
            attend(i)

    lax.fori_loop(2 * PIECES + 2, steps + 2, rest, 0)

    key_sums = jnp.dot(
        member[...], qkv[:, HS : 2 * HS], preferred_element_type=jnp.float32
    )
    share = 0.75 * key_sums / jnp.maximum(counts[...], 1.0)
    for i in range(n):
        cent_out[i] = share[i * owned : (i + 1) * owned, :]

    def cent_copy(i):
        return remote(cent_out.at[i], cent_in.at[z], cent_send.at[i], cent_recv.at[z], (g, i, h))

    for i in range(n):
        @pl.when(i != z)
        def _():
            cent_copy(i).start()

    @pl.when(z >= n // 2)
    def _():
        for i in range(1, n - 1):
            attend(i)

    attend(n - 1)

    ctx_ref[:, col(z)] = ctx_out[pl.ds(pl.multiple_of(z * block, block), block), :]
    cent_in[z] = cent_out[z]

    for i in range(n):
        @pl.when(i != z)
        def _():
            remote(cent_out.at[i], cent_in.at[i], cent_send.at[i], cent_recv.at[i], (g, i, h)).wait_recv()
    new_ref[...] = 0.25 * cent_ref[...] + cent_in[...]

    for j in range(3):
        for d in range(1, n):
            w_copy(d, j).wait_send()
            w_forward(d, j).wait_send()
    for d in range(1, n):
        ids_copy(d).wait_send()

    @pl.when(z < n - 1)
    def _():
        for p in range(PIECES):
            own_copy(p, True).wait_send()

    @pl.when(z > 0)
    def _():
        for p in range(PIECES):
            own_copy(p, False).wait_send()

    def drain(t, carry):
        src, p = split(t)

        @pl.when(along_exists(src))
        def _():
            along(src, p).wait_send()

        across(src, p, quarter).wait_send()
        beside(src, p, 0, quarter).wait_send()
        beside(src, p, 1, other_x).wait_send()
        return carry

    lax.fori_loop(0, steps, drain, 0)
    for i in range(n):
        @pl.when(i != z)
        def _():
            cent_copy(i).wait_send()
            context_copy(i).wait_send()
            remote(
                ctx_out.at[pl.ds(i * block, block), :], ctx_ref.at[:, pl.ds(i * HS, HS)],
                ctx_send.at[i], ctx_recv.at[i], (g, i, h),
            ).wait_recv()


def by_head(tokens, proj_weight, cluster_ids, centroids):
    n = lax.axis_size("seq")
    block, width = tokens.shape
    heads = cluster_ids.shape[0]
    owned = centroids.shape[1]
    ids = jnp.broadcast_to(cluster_ids.reshape(heads, 1, block), (heads, 8, block))
    dma = pltpu.SemaphoreType.DMA
    return tuple(
        pl.pallas_call(
            kernel,
            out_shape=(
                jax.ShapeDtypeStruct((block, heads * HS), jnp.bfloat16),
                jax.ShapeDtypeStruct((heads, owned, HS), jnp.float32),
            ),
            in_specs=[pl.BlockSpec(memory_space=pl.ANY)] * 3 + [pl.BlockSpec(memory_space=pltpu.VMEM)],
            out_specs=(pl.BlockSpec(memory_space=pltpu.VMEM), pl.BlockSpec(memory_space=pltpu.VMEM)),
            scratch_shapes=[
                pltpu.VMEM((n * block, width), jnp.bfloat16),
                pltpu.VMEM((width, 3 * HS), jnp.bfloat16),
                pltpu.VMEM((n * block, 3 * HS), jnp.bfloat16),
                pltpu.VMEM((8, n * block), jnp.int32),
                pltpu.VMEM((n * block, HS), jnp.float32),
                pltpu.VMEM((n * owned, n * block), jnp.bfloat16),
                pltpu.VMEM((n * owned, HS), jnp.float32),
                pltpu.VMEM((n * block, HS), jnp.bfloat16),
                pltpu.VMEM((n, owned, HS), jnp.float32),
                pltpu.VMEM((n, owned, HS), jnp.float32),
                dma((5,)),
                dma((n - 1,)), dma((n - 1,)),
                dma((n - 1, 3)), dma((n - 1, 3)),
                dma((n - 1, 3)), dma((n - 1, 3)),
                dma((2, n, PIECES)), dma((n, PIECES)),
                dma((n, PIECES)), dma((n, PIECES)),
                dma((2, n, PIECES)), dma((2, n, PIECES)),
                dma((n,)), dma((n,)),
                dma((n,)), dma((n,)),
            ],
            compiler_params=pltpu.CompilerParams(
                collective_id=0, has_side_effects=True, vmem_limit_bytes=58 << 20
            ),
        )(tokens, proj_weight, ids, centroids)
    )


def local(tokens, proj_weight, cluster_ids, centroids):
    heads = cluster_ids.shape[0]
    fits = (
        lax.axis_size("seq") == heads == 4
        and lax.axis_size("head") == 4
        and lax.axis_size("groups") == 2
        and tokens.shape[0] % ROWS == 0
    )
    return (by_head if fits else general)(tokens, proj_weight, cluster_ids, centroids)


def solution(mesh):
    return jax.shard_map(
        local,
        mesh=mesh,
        in_specs=(
            P(("groups", "seq"), None),
            P(None, "seq", "head"),
            P("head", ("groups", "seq"), None),
            P(("groups", "head"), "seq", None),
        ),
        out_specs=(P(("groups", "seq"), "head"), P(("groups", "head"), "seq", None)),
        check_vma=False,
    )
```

```python
import functools

import jax
import jax.numpy as jnp
from jax import lax
from jax.experimental import pallas as pl
from jax.experimental.pallas import tpu as pltpu
from jax.sharding import PartitionSpec as P

HS = 128
CLUSTERS = 256
SLOTS = 4


def general(tokens, proj_weight, cluster_ids, centroids):
    owners = lax.axis_size("seq")
    local_rows = tokens.shape[0]
    columns = proj_weight.shape[2]
    head_count = columns // HS
    owned = CLUSTERS // owners
    capacity = owners * SLOTS
    score_scale = HS ** (-0.5)
    projected = jnp.einsum(
        "td,pdc->ptc",
        tokens,
        lax.all_gather(proj_weight, "seq", axis=1, tiled=True),
        preferred_element_type=jnp.float32,
    ).astype(jnp.bfloat16)
    per_head = projected.reshape(3, local_rows, head_count, HS).transpose(2, 1, 0, 3)
    packed = per_head.reshape(head_count, local_rows, 3 * HS)
    member = cluster_ids[:, :, 0]
    labels = jnp.arange(CLUSTERS, dtype=jnp.int32)
    onehot = (member[:, :, None] == labels[None, None, :]).astype(jnp.bfloat16)
    ordinal_rows = jnp.arange(local_rows, dtype=jnp.int32)
    earlier = (ordinal_rows[None, :] < ordinal_rows[:, None]).astype(jnp.bfloat16)
    before = jnp.einsum("ts,hsc->htc", earlier, onehot, preferred_element_type=jnp.float32)
    ranking = jnp.take_along_axis(before, member[:, :, None], axis=2)[:, :, 0].astype(jnp.int32)
    placed = member * SLOTS + ranking
    head_index = jnp.arange(head_count, dtype=jnp.int32)[:, None]
    outbox = (
        jnp.zeros((head_count, CLUSTERS * SLOTS, 3 * HS), jnp.bfloat16)
        .at[head_index, placed]
        .set(packed)
    )
    outbox = outbox.reshape(head_count, owners, owned * SLOTS, 3 * HS)
    local_counts = jnp.sum(onehot, axis=1, dtype=jnp.float32)
    tallies = local_counts.astype(jnp.int32).reshape(head_count, owners, owned)
    blocks = lax.all_to_all(outbox, "seq", split_axis=1, concat_axis=1, tiled=True)
    arrived = lax.all_to_all(tallies, "seq", split_axis=1, concat_axis=1, tiled=True)
    local_heads = blocks.shape[0]
    arranged = (
        blocks.reshape(local_heads, owners, owned, SLOTS, 3 * HS)
        .transpose(0, 2, 1, 3, 4)
        .reshape(local_heads, owned, capacity, 3 * HS)
    )
    filled = jnp.arange(SLOTS, dtype=jnp.int32)[None, None, None, :] < arrived[:, :, :, None]
    filled = filled.transpose(0, 2, 1, 3).reshape(local_heads, owned, capacity)
    queries = arranged[:, :, :, :HS]
    key_block = arranged[:, :, :, HS : 2 * HS]
    value_block = arranged[:, :, :, 2 * HS :]
    scores = (
        jnp.einsum("hcqd,hckd->hcqk", queries, key_block, preferred_element_type=jnp.float32)
        * score_scale
    )
    ordinal = jnp.arange(capacity, dtype=jnp.int32)
    causal = ordinal[None, None, None, :] <= ordinal[None, None, :, None]
    itself = ordinal[None, None, None, :] == ordinal[None, None, :, None]
    allowed = filled[:, :, None, :] & causal | itself
    scores = jnp.where(allowed, scores, -1e30)
    row_max = jnp.max(scores, axis=3, keepdims=True)
    raised = jnp.exp(scores - row_max)
    weights = (raised / jnp.sum(raised, axis=3, keepdims=True)).astype(jnp.bfloat16)
    attended = jnp.einsum(
        "hcqk,hckd->hcqd", weights, value_block, preferred_element_type=jnp.float32
    ).astype(jnp.bfloat16)
    attended = (
        attended.reshape(local_heads, owned, owners, SLOTS, HS)
        .transpose(0, 2, 1, 3, 4)
        .reshape(local_heads, owners, owned * SLOTS, HS)
    )
    returned = lax.all_to_all(attended, "seq", split_axis=1, concat_axis=1, tiled=True)
    key_sums = jnp.einsum(
        "hck,hckd->hcd", filled.astype(jnp.bfloat16), key_block, preferred_element_type=jnp.float32
    )
    counts = jnp.sum(filled, axis=2).astype(jnp.float32)
    exchanged = (returned, key_sums, counts)
    returned, key_sums, counts = exchanged
    gathered = returned.reshape(head_count, CLUSTERS * SLOTS, HS)
    mine = jax.vmap(lambda table, where: table[where])(gathered, placed)
    context = mine.transpose(1, 0, 2).reshape(local_rows, head_count * HS)
    updated = 0.25 * centroids + 0.75 * key_sums / jnp.maximum(counts, 1.0)[:, :, None]
    return (context, updated)


MESH = pl.DeviceIdType.MESH
PIECES = 4
ROWS = 256
QROWS = 256


def kernel(
    tok_hbm, w_hbm, ids_hbm, ctx_ref, new_ref,
    tok, w, qkv, ids, ids_col, member, counts, ctx_out, cent_out, cent_in,
    local_sem, ids_send, ids_recv, wz_send, wz_recv, wy_send, wy_recv,
    z_send, z_recv, x_send, x_recv, c_send, c_recv, ctx_send, ctx_recv, cent_send, cent_recv,
):
    g = lax.axis_index("groups")
    z = lax.axis_index("seq")
    h = lax.axis_index("head")
    n = lax.axis_size("seq")
    block = tok_hbm.shape[0]
    depth = w_hbm.shape[1]
    half = depth // 2
    piece = block // PIECES // 4
    group = block // PIECES
    quarter = h
    over_x = (g, z, lax.rem(h + 2, 4))
    over_c = (g, z, h + 1 - 2 * lax.rem(h, 2))
    over_y = (1 - g, z, h)

    barrier = pltpu.get_barrier_semaphore()
    for d in range(1, n):
        pl.semaphore_signal(barrier, inc=1, device_id=(g, lax.rem(z + d, n), h), device_id_type=MESH)
    for peer in (over_x, over_c, over_y):
        pl.semaphore_signal(barrier, inc=1, device_id=peer, device_id_type=MESH)
    pl.semaphore_wait(barrier, n + 2)

    def remote(src, dst, send, recv, device):
        return pltpu.make_async_remote_copy(
            src_ref=src, dst_ref=dst, send_sem=send, recv_sem=recv, device_id=device, device_id_type=MESH
        )

    def col(j):
        return pl.ds(pl.multiple_of(j * HS, HS), HS)

    def rows_of(src, p, q):
        return pl.ds(pl.multiple_of(src * block + p * group + q * piece, piece), piece)

    def w_copy(d, j):
        to = lax.rem(z + d, n)
        return remote(
            w_hbm.at[j, pl.ds(pl.multiple_of(g * half, half), half), col(to)],
            w.at[pl.ds(pl.multiple_of(z * depth + g * half, half), half), pl.ds(j * HS, HS)],
            wz_send.at[d - 1, j], wz_recv.at[d - 1, j], (g, to, h),
        )

    def w_arrived(d, j):
        src = lax.rem(z - d + n, n)
        part = w.at[pl.ds(pl.multiple_of(src * depth + g * half, half), half), pl.ds(j * HS, HS)]
        return part

    def ids_copy(d):
        to = lax.rem(z + d, n)
        return remote(
            ids_hbm.at[to], ids.at[0:1, pl.ds(pl.multiple_of(z * block, block), block)],
            ids_send.at[d - 1], ids_recv.at[d - 1], (g, to, h),
        )

    for d in range(1, n):
        ids_copy(d).start()

    def own_copy(p, up):
        to = z + 1 if up else z - 1
        return remote(
            tok_hbm.at[pl.ds(pl.multiple_of(p * group + quarter * piece, piece), piece), :],
            tok.at[rows_of(z, p, quarter), :],
            z_send.at[1 if up else 0, z, p], z_recv.at[z, p], (g, to, h),
        )

    def own_start(up):
        for p in range(PIECES):
            own_copy(p, up).start()

    for p in range(max(3, PIECES)):
        if p < PIECES:
            pl.when(z == 1)(lambda: own_copy(p, False).start())
            pl.when(z == n - 2)(lambda: own_copy(p, True).start())
        if p < 3:
            for d in range(1, n):
                w_copy(d, p).start()
    pl.when((z != 1) & (z < n - 2))(lambda: own_start(True))
    pl.when(z > 1)(lambda: own_start(False))

    locals_ = [
        pltpu.make_async_copy(tok_hbm, tok.at[pl.ds(pl.multiple_of(z * block, block), block), :], local_sem.at[0]),
        pltpu.make_async_copy(ids_hbm.at[z], ids.at[0:1, pl.ds(pl.multiple_of(z * block, block), block)], local_sem.at[1]),
    ]
    for j in range(3):
        locals_.append(
            pltpu.make_async_copy(
                w_hbm.at[j, :, col(z)],
                w.at[pl.ds(pl.multiple_of(z * depth, depth), depth), pl.ds(j * HS, HS)],
                local_sem.at[2 + j],
            )
        )
    for copy in locals_:
        copy.start()

    def w_forward(d, j):
        part = w_arrived(d, j)
        return remote(part, part, wy_send.at[d - 1, j], wy_recv.at[d - 1, j], over_y)

    def w_step(j):
        for d in range(1, n):
            w_copy(d, j).wait_recv()
            w_forward(d, j).start()

    def project(start):
        rows = pl.ds(pl.multiple_of(start, ROWS), ROWS)
        qkv[rows, :] = jnp.dot(tok[rows, :], w[...], preferred_element_type=jnp.float32).astype(jnp.bfloat16)

    def source(s):
        low = s + (s >= z).astype(jnp.int32)
        high = jnp.where(s == 0, 2 * n - 3 - z, s - 1)
        return jnp.where(z < n // 2, low, high)

    def split(t):
        return source(t // PIECES), lax.rem(t, PIECES)

    def along(src, p):
        up = (src < z).astype(jnp.int32)
        part = tok.at[rows_of(src, p, quarter), :]
        return remote(part, part, z_send.at[up, src, p], z_recv.at[src, p], (g, z + 2 * up - 1, h))

    def along_exists(src):
        return jnp.where(src < z, z < n - 1, z > 0)

    def across(src, p, q):
        part = tok.at[rows_of(src, p, q), :]
        return remote(part, part, x_send.at[src, p], x_recv.at[src, p], over_x)

    def beside(src, p, which, q):
        part = tok.at[rows_of(src, p, q), :]
        return remote(part, part, c_send.at[which, src, p], c_recv.at[which, src, p], over_c)

    other_x = lax.rem(h + 2, 4)
    sib = h + 1 - 2 * lax.rem(h, 2)
    sib_x = lax.rem(sib + 2, 4)
    steps = (n - 1) * PIECES

    inner = (z > 0) & (z < n - 1)

    def carry_on(t):
        src, p = split(t)
        along(src, p).wait_recv()

        @pl.when(along_exists(src))
        def _():
            along(src, p).start()

        across(src, p, quarter).start()
        beside(src, p, 0, quarter).start()

    def hand_over(t):
        src, p = split(t)
        across(src, p, other_x).wait_recv()
        beside(src, p, 1, other_x).start()

    def complete(t):
        src, p = split(t)
        beside(src, p, 0, sib).wait_recv()
        beside(src, p, 1, sib_x).wait_recv()
        return src, p

    for d in range(1, n):
        ids_copy(d).wait_recv()
    for copy in locals_[:2]:
        copy.wait()
    total = n * block
    for i in range(total // 128):
        row = ids[0:1, i * 128 : (i + 1) * 128].astype(jnp.float32)
        ids_col[i * 128 : (i + 1) * 128, :] = jnp.broadcast_to(row, (128, 128)).T
    owned = cent_in.shape[1]
    clusters = owned * n
    labels = lax.broadcasted_iota(jnp.int32, (clusters, total), 0)
    named = (labels == ids[0:1, :]).astype(jnp.float32)
    counts[...] = jnp.broadcast_to(jnp.sum(named, axis=1, keepdims=True), counts.shape)
    member[...] = named.astype(jnp.bfloat16)

    for t in range(max(3, PIECES)):
        if t < 3:
            pl.when(inner)(lambda: w_step(t))
        if t < PIECES:
            carry_on(t)
        if t < 3:
            pl.when(~inner)(lambda: w_step(t))
        if 1 <= t < PIECES:
            hand_over(t - 1)
        if 2 <= t < PIECES:
            complete(t - 2)

    pl.when(z == 1)(lambda: own_start(True))

    def rest(t, carry):
        pl.when(t < steps)(lambda: carry_on(t))
        pl.when(t < steps + 1)(lambda: hand_over(t - 1))
        src, p = complete(t - 2)

        @pl.when((t >= PIECES + 2) & (lax.rem((p + 1) * group, ROWS) == 0))
        def _():
            project(src * block + (p + 1) * group - ROWS)

        return carry

    lax.fori_loop(PIECES, PIECES + 2, rest, 0)

    for j in range(3):
        for d in range(1, n):
            src = lax.rem(z - d + n, n)
            part = w.at[pl.ds(pl.multiple_of(src * depth + (1 - g) * half, half), half), pl.ds(j * HS, HS)]
            remote(part, part, wy_send.at[d - 1, j], wy_recv.at[d - 1, j], over_y).wait_recv()
    for copy in locals_[2:]:
        copy.wait()

    def early_rows(i, carry):
        which = jnp.where(i < block // ROWS, z, source(0))
        project(which * block + lax.rem(i, block // ROWS) * ROWS)
        return carry

    lax.fori_loop(0, 2 * (block // ROWS), early_rows, 0)
    scale = HS ** (-0.5)

    def context_copy(i):
        return remote(
            ctx_out.at[pl.ds(i * block, block), :], ctx_ref.at[:, col(z)],
            ctx_send.at[i], ctx_recv.at[z], (g, i, h),
        )

    def attend(i):
        length = (i + 1) * block
        key_ids = ids[0:1, 0:length].astype(jnp.float32)

        def body(b, carry):
            start = pl.multiple_of(i * block + b * QROWS, QROWS)
            rows = pl.ds(start, QROWS)
            scores = lax.dot_general(
                qkv[rows, 0:HS], qkv[0:length, HS : 2 * HS], (((1,), (1,)), ((), ())),
                preferred_element_type=jnp.float32,
            ) * scale
            at_query = start + lax.broadcasted_iota(jnp.int32, (QROWS, length), 0)
            at_key = lax.broadcasted_iota(jnp.int32, (QROWS, length), 1)
            allowed = (ids_col[rows, 0:1] == key_ids) & (at_key <= at_query)
            scores = jnp.where(allowed, scores, -1e30)
            raised = jnp.exp(scores - jnp.max(scores, axis=1, keepdims=True))
            inverse = 1.0 / jnp.sum(raised, axis=1, keepdims=True)
            weights = (raised * inverse).astype(jnp.bfloat16)
            ctx_out[rows, :] = jnp.dot(
                weights, qkv[0:length, 2 * HS : 3 * HS], preferred_element_type=jnp.float32
            ).astype(jnp.bfloat16)
            return carry

        lax.fori_loop(0, block // QROWS, body, 0)

        @pl.when(i != z)
        def _():
            context_copy(i).start()

    lax.fori_loop(PIECES + 2, 2 * PIECES + 2, rest, 0)
    attend(0)

    @pl.when(z < n // 2)
    def _():
        for i in range(1, n - 1):
            attend(i)

    lax.fori_loop(2 * PIECES + 2, steps + 2, rest, 0)

    key_sums = jnp.dot(
        member[...], qkv[:, HS : 2 * HS], preferred_element_type=jnp.float32
    )
    share = 0.75 * key_sums / jnp.maximum(counts[...], 1.0)
    for i in range(n):
        cent_out[i] = share[i * owned : (i + 1) * owned, :]

    def cent_copy(i):
        return remote(cent_out.at[i], cent_in.at[z], cent_send.at[i], cent_recv.at[z], (g, i, h))

    for i in range(n):
        @pl.when(i != z)
        def _():
            cent_copy(i).start()

    @pl.when(z >= n // 2)
    def _():
        for i in range(1, n - 1):
            attend(i)

    attend(n - 1)

    ctx_ref[:, col(z)] = ctx_out[pl.ds(pl.multiple_of(z * block, block), block), :]
    cent_in[z] = cent_out[z]

    for i in range(n):
        @pl.when(i != z)
        def _():
            remote(cent_out.at[i], cent_in.at[i], cent_send.at[i], cent_recv.at[i], (g, i, h)).wait_recv()
    new_ref[...] = cent_in[...]

    for j in range(3):
        for d in range(1, n):
            w_copy(d, j).wait_send()
            w_forward(d, j).wait_send()
    for d in range(1, n):
        ids_copy(d).wait_send()

    @pl.when(z < n - 1)
    def _():
        for p in range(PIECES):
            own_copy(p, True).wait_send()

    @pl.when(z > 0)
    def _():
        for p in range(PIECES):
            own_copy(p, False).wait_send()

    def drain(t, carry):
        src, p = split(t)

        @pl.when(along_exists(src))
        def _():
            along(src, p).wait_send()

        across(src, p, quarter).wait_send()
        beside(src, p, 0, quarter).wait_send()
        beside(src, p, 1, other_x).wait_send()
        return carry

    lax.fori_loop(0, steps, drain, 0)
    for i in range(n):
        @pl.when(i != z)
        def _():
            cent_copy(i).wait_send()
            context_copy(i).wait_send()
            remote(
                ctx_out.at[pl.ds(i * block, block), :], ctx_ref.at[:, pl.ds(i * HS, HS)],
                ctx_send.at[i], ctx_recv.at[i], (g, i, h),
            ).wait_recv()


def finish(context_ref, share_ref, cent_ref, ctx_ref, new_ref):
    ctx_ref[...] = context_ref[...]
    new_ref[...] = 0.25 * cent_ref[...] + share_ref[...]


def by_head(tokens, proj_weight, cluster_ids, centroids):
    n = lax.axis_size("seq")
    block, width = tokens.shape
    heads = cluster_ids.shape[0]
    owned = centroids.shape[1]
    ids = cluster_ids.reshape(heads, 1, block)
    dma = pltpu.SemaphoreType.DMA
    context, share = (
        pl.pallas_call(
            kernel,
            out_shape=(
                jax.ShapeDtypeStruct((block, heads * HS), jnp.bfloat16),
                jax.ShapeDtypeStruct((heads, owned, HS), jnp.float32),
            ),
            in_specs=[pl.BlockSpec(memory_space=pl.ANY)] * 3,
            out_specs=(pl.BlockSpec(memory_space=pltpu.VMEM), pl.BlockSpec(memory_space=pltpu.VMEM)),
            scratch_shapes=[
                pltpu.VMEM((n * block, width), jnp.bfloat16),
                pltpu.VMEM((width, 3 * HS), jnp.bfloat16),
                pltpu.VMEM((n * block, 3 * HS), jnp.bfloat16),
                pltpu.VMEM((8, n * block), jnp.int32),
                pltpu.VMEM((n * block, HS), jnp.float32),
                pltpu.VMEM((n * owned, n * block), jnp.bfloat16),
                pltpu.VMEM((n * owned, HS), jnp.float32),
                pltpu.VMEM((n * block, HS), jnp.bfloat16),
                pltpu.VMEM((n, owned, HS), jnp.float32),
                pltpu.VMEM((n, owned, HS), jnp.float32),
                dma((5,)),
                dma((n - 1,)), dma((n - 1,)),
                dma((n - 1, 3)), dma((n - 1, 3)),
                dma((n - 1, 3)), dma((n - 1, 3)),
                dma((2, n, PIECES)), dma((n, PIECES)),
                dma((n, PIECES)), dma((n, PIECES)),
                dma((2, n, PIECES)), dma((2, n, PIECES)),
                dma((n,)), dma((n,)),
                dma((n,)), dma((n,)),
            ],
            compiler_params=pltpu.CompilerParams(
                collective_id=0, has_side_effects=True, vmem_limit_bytes=58 << 20
            ),
        )(tokens, proj_weight, ids)
    )
    return tuple(
        pl.pallas_call(
            finish,
            out_shape=(
                jax.ShapeDtypeStruct(context.shape, context.dtype),
                jax.ShapeDtypeStruct(centroids.shape, centroids.dtype),
            ),
            compiler_params=pltpu.CompilerParams(vmem_limit_bytes=8 << 20),
        )(context, share, centroids)
    )


def local(tokens, proj_weight, cluster_ids, centroids):
    heads = cluster_ids.shape[0]
    fits = (
        lax.axis_size("seq") == heads == 4
        and lax.axis_size("head") == 4
        and lax.axis_size("groups") == 2
        and tokens.shape[0] % ROWS == 0
    )
    return (by_head if fits else general)(tokens, proj_weight, cluster_ids, centroids)


def solution(mesh):
    return jax.shard_map(
        local,
        mesh=mesh,
        in_specs=(
            P(("groups", "seq"), None),
            P(None, "seq", "head"),
            P("head", ("groups", "seq"), None),
            P(("groups", "head"), "seq", None),
        ),
        out_specs=(P(("groups", "seq"), "head"), P(("groups", "head"), "seq", None)),
        check_vma=False,
    )
```
